32 devices in a mesh: dp: 16 (over z, y, x), tensor: 2 (over core).
Axes of the slice: x: 2, y: 2, z: 4, core: 2. Of those that a mesh axis runs over, the one named last changes fastest.
Arguments:
- block_input: bfloat16 [4096, 2048], P(('dp', 'tensor')), may hold values from -6 to 6
- attn_gain: bfloat16 [2048], P('dp'), may hold values from 0.25 to 1.75
- qkv_weight: bfloat16 [2048, 3, 8, 128], P('dp', None, 'tensor'), may hold values from -0.125 to 0.125
- qkv_bias: bfloat16 [3, 8, 128], P(None, 'tensor', 'dp'), may hold values from -6 to 6
- out_weight: bfloat16 [8, 128, 2048], P('tensor', None, 'dp'), may hold values from -0.375 to 0.375
- ffn_gain: bfloat16 [2048], P('dp'), may hold values from 0.25 to 1.75
- shared_in: bfloat16 [2048, 2, 2816], P('dp', None, 'tensor'), may hold values from -0.125 to 0.125
- shared_out: bfloat16 [2816, 2048], P('tensor', 'dp'), may hold values from -0.109375 to 0.109375
- shared_gate: bfloat16 [2048], P('dp'), may hold values from -0.125 to 0.125
- expert_in: bfloat16 [16, 2048, 2, 704], P('dp', None, None, 'tensor'), may hold values from -0.125 to 0.125
- expert_out: bfloat16 [16, 704, 2048], P('dp', 'tensor'), may hold values from -0.21875 to 0.21875
- expert_picks: int32 [4096, 4], P('dp'), may hold values from 0 to 15, all different within a row; in each aligned block of 256 rows (0 to 255, 256 to 511, ...) at most 96 rows name the same one
- expert_gates: float32 [4096, 4], P('dp'), may hold values from 0.2 to 1
- segment_ids: int32 [16, 256], P('dp'), may hold values from 0 to 7, never falling along the last dimension, each value on 1 to 128 neighbouring positions
- output_grad: bfloat16 [4096, 2048], P(('dp', 'tensor')), may hold values from -6 to 6
Outputs:
- block_output: bfloat16 [4096, 2048], P(('dp', 'tensor'))
- input_grad: float32 [4096, 2048], P(('dp', 'tensor'))
- attn_gain_grad: float32 [2048], P('dp')
- qkv_weight_grad: float32 [2048, 3, 8, 128], P('dp', None, 'tensor')
- qkv_bias_grad: float32 [3, 8, 128], P(None, 'tensor', 'dp')
- out_weight_grad: float32 [8, 128, 2048], P('tensor', None, 'dp')
- ffn_gain_grad: float32 [2048], P('dp')
- shared_in_grad: float32 [2048, 2, 2816], P('dp', None, 'tensor')
- shared_out_grad: float32 [2816, 2048], P('tensor', 'dp')
- shared_gate_grad: float32 [2048], P('dp')
- expert_in_grad: float32 [16, 2048, 2, 704], P('dp', None, None, 'tensor')
- expert_out_grad: float32 [16, 704, 2048], P('dp', 'tensor')
The draws below stay inside these ranges and needn't reach their ends.
Inputs may be any that keep to these rules, and one draw needn't show every extreme that they name: `expert_picks`: the 4 picks of a token differ. Within the 256 tokens of one row no expert is picked more than 96 times, and some expert is picked exactly 96 times in some row. `segment_ids`: segment numbers never fall along a row; each segment holds 1 to 128 positions.
All inputs are finite; a program needn't handle non-finite values.
Results may differ from the reference program's by a relative error of at most 0.04.
Values may be sent and summed in bfloat16 or wider, within the bound.
No kernel may reach another device: no remote copies, remote signals or barrier semaphores. Data moves between devices by JAX's collectives and lax.ppermute only.
A program may use at most 256 MiB of HBM per device.

```python
import math
import jax
import jax.numpy as jnp
import numpy as np
from jax import lax

D = 2048
HEADS = 8
HEAD_DIM = 128
EXPERT_UNITS = 704
SHARED_UNITS = 2816
TOPK = 4
LEN = 256
EXPERTS = 16
CAP = 96
ROWS = 16
TOKENS = 4096
N_DP = 16
N_TENSOR = 2


def draw_qkv_bias(key, part):
    base_key = jax.random.fold_in(key, 11)
    drawn = jnp.clip(0.5 * jax.random.normal(base_key, (3, HEADS, HEAD_DIM), jnp.float32), -3.0, 3.0)
    return drawn.astype(jnp.bfloat16)


def shard_levels(key, dims, split, least, top_value):
    level = 1.0
    for dim, blocks in split:
        heights = jax.random.uniform(jax.random.fold_in(jax.random.fold_in(key, 6), dim), (blocks,), jnp.float32, least / len(split), top_value / len(split))
        level = level * jnp.repeat(jnp.exp(heights), dims[dim] // blocks).reshape((-1,) + (1,) * (len(dims) - 1 - dim))
    return level


def length_profile(number_of, total, most, slope):
    weights = [(1 << 20) // math.isqrt(rank ** slope) + 1 for rank in range(2, number_of + 1)]
    surplus, counts = total - most - (number_of - 1), [1] * (number_of - 1)
    while surplus > 0:
        movable = [i for i in range(number_of - 1) if counts[i] < most]
        mass, remaining = sum([weights[i] for i in movable]), surplus
        for i in movable:
            addition = min(most - counts[i], max(1, remaining * weights[i] // mass), surplus)
            counts[i] = counts[i] + addition
            surplus = surplus - addition
    return np.array([most] + counts)


def ragged_sizes(key, count, total, reach, skew):
    if count == 2:
        one = jax.random.randint(key, (), max(1, total - reach), min(reach, total - 1) + 1)
        return jnp.stack([one, total - one])
    tallies = jnp.asarray(length_profile(count, total, reach, skew), jnp.int32)
    couples = (count - 1) // 2
    donor, taker = tallies[1:1 + 2 * couples:2], tallies[2:2 + 2 * couples:2]
    slack = jnp.minimum(donor - 1, reach - taker)
    passed = jax.random.randint(jax.random.fold_in(key, 1), (couples,), 0, 1 << 20) % (slack + 1)
    tallies = tallies.at[1:1 + 2 * couples:2].set(donor - passed).at[2:2 + 2 * couples:2].set(taker + passed)
    return tallies[jax.random.permutation(jax.random.fold_in(key, 2), count)]


def assign_block(stream_key, own, number, rows, amount, top, limit, skew):
    sequence = jax.random.permutation(stream_key, amount)
    crowded, common = portions_of(amount, rows * top, limit, skew, True), portions_of(amount, rows * top, limit, skew, False)
    places = jnp.arange(amount)

    def named(lengths, turn):
        used = int((lengths > 0).sum())
        fixed = max(1, used // 4)
        moved = fixed + (places - fixed + turn * (used - fixed)) % max(1, amount - fixed)
        return jnp.zeros((amount,), jnp.int32).at[sequence[jnp.where(places < fixed, places, moved)]].set(jnp.asarray(lengths, jnp.int32))

    lengths = jnp.where(number % 4 == 0, named(crowded, number // 4), named(common, number - number // 4 - 1))
    mixed = jax.random.permutation(jax.random.fold_in(own, 3), amount)
    donor, sink = mixed[0:amount // 2 * 2:2], mixed[1:amount // 2 * 2:2]
    slack = jnp.minimum(lengths[donor] - 1, limit - lengths[sink]) // 2
    slack = jnp.where((donor == sequence[0]) | (sink == sequence[0]) | (lengths[sink] == 0), 0, jnp.maximum(slack, 0))
    moved = jax.random.randint(jax.random.fold_in(own, 4), (amount // 2,), 0, 1 << 20) % (slack + 1)
    lengths = lengths.at[donor].add(-moved).at[sink].add(moved)
    members = jnp.searchsorted(jnp.cumsum(lengths), jnp.arange(rows * top), side="right").astype(jnp.int32)
    grid = members.reshape(top, rows).T
    grid = grid[jax.random.permutation(jax.random.fold_in(own, 1), rows)]
    turn = jax.random.randint(jax.random.fold_in(own, 2), (rows, 1), 0, top)
    return jnp.take_along_axis(grid, (jnp.arange(top)[None, :] + turn) % top, axis=1)


def portions_of(count, total, bound, slope, full):
    loads = [(1 << 20) // math.isqrt(rank ** slope) + 1 for rank in range(1, count + 1)]
    largest = bound if full else min(bound, max(-(-total // count), total * loads[0] // sum(loads)))
    least = 1 if total - largest >= count - 1 else 0
    holding, surplus = [largest] + [least] * (count - 1), total - largest - least * (count - 1)
    while surplus > 0:
        movable = [i for i in range(1, count) if holding[i] < largest] or [i for i in range(1, count) if holding[i] < bound]
        whole, left = sum([loads[i] for i in movable]), surplus
        for i in movable:
            extra = min(bound - holding[i], max(1, left * loads[i] // whole), surplus)
            holding[i] = holding[i] + extra
            surplus = surplus - extra
    return np.array(holding)


def bell_draw(stream_key, dims, deviation, most, shards=(), held_as=jnp.bfloat16):
    level = shard_levels(stream_key, dims, shards, -0.22, 0.18) if shards else 1.0
    array = jax.random.normal(stream_key, dims, jnp.float32) * deviation * level
    return jnp.minimum(jnp.maximum(array, -most), most).astype(held_as)


def setup_inputs(seed: int = 0) -> dict:
    keys = jax.random.split(jax.random.key(seed), 16)
    block_input = bell_draw(keys[0], (TOKENS, D), 1.0, 6.0, ((0, 32),))
    attn_gain = jnp.clip(1.0 + 0.15 * jax.random.normal(keys[1], (D,), jnp.float32), 0.25, 1.75).astype(jnp.bfloat16)
    qkv_weight = bell_draw(keys[2], (D, 3, HEADS, HEAD_DIM), D ** -0.5, 0.125, ((0, 16), (2, 2)))
    qkv_bias = draw_qkv_bias(jax.random.fold_in(keys[15], 71), 0)
    out_weight = bell_draw(keys[4], (HEADS, HEAD_DIM, D), (D // 8) ** -0.5, 0.375, ((0, 2), (2, 16)))
    ffn_gain = jnp.clip(1.0 + 0.15 * jax.random.normal(keys[5], (D,), jnp.float32), 0.25, 1.75).astype(jnp.bfloat16)
    shared_in = bell_draw(keys[6], (D, 2, SHARED_UNITS), D ** -0.5, 0.125, ((0, 16), (2, 2)))
    shared_out = bell_draw(keys[7], (SHARED_UNITS, D), SHARED_UNITS ** -0.5, 0.109375, ((0, 2), (1, 16)))
    shared_gate = bell_draw(keys[8], (D,), D ** -0.5, 0.125, ((0, 16),))
    expert_in = bell_draw(keys[9], (EXPERTS, D, 2, EXPERT_UNITS), D ** -0.5, 0.125, ((0, 16), (3, 2)))
    expert_out = bell_draw(keys[10], (EXPERTS, EXPERT_UNITS, D), EXPERT_UNITS ** -0.5, 0.21875, ((0, 16), (1, 2)))
    expert_picks_keys = jax.random.split(jax.random.fold_in(keys[11], 1), TOKENS // LEN)
    expert_picks_turns = jax.random.permutation(jax.random.fold_in(keys[11], 3), TOKENS // LEN)
    expert_picks = jax.vmap(lambda own, number: assign_block(jax.random.fold_in(keys[11], 2), own, number, LEN, EXPERTS, TOPK, CAP, 2))(expert_picks_keys, expert_picks_turns).reshape((TOKENS, TOPK))
    expert_gates = jnp.clip(jnp.exp(math.log(1.0) - 1.609438 * jax.random.uniform(keys[12], (TOKENS, TOPK), jnp.float32) ** shard_levels(keys[12], (TOKENS, TOPK), ((0, 16),), -0.2, 0.2)), 0.2, 1.0)
    segment_ids = jax.vmap(lambda own: jnp.searchsorted(jnp.cumsum(ragged_sizes(own, max(4, LEN // 32), LEN, LEN // 2, 1)), jnp.arange(LEN), side="right"))(jax.random.split(keys[13], ROWS)).reshape((ROWS, LEN)).astype(jnp.int32)
    output_grad = bell_draw(keys[14], (TOKENS, D), 1.0, 6.0, ((0, 32),))
    return {"block_input": block_input, "attn_gain": attn_gain, "qkv_weight": qkv_weight, "qkv_bias": qkv_bias, "out_weight": out_weight, "ffn_gain": ffn_gain, "shared_in": shared_in, "shared_out": shared_out, "shared_gate": shared_gate, "expert_in": expert_in, "expert_out": expert_out, "expert_picks": expert_picks, "expert_gates": expert_gates, "segment_ids": segment_ids, "output_grad": output_grad}


norm_epsilon = 1e-06

def mix(form, left, right):
    return jnp.einsum(form, left.astype(jnp.float32), right.astype(jnp.float32))

def rms_scale(values):
    return lax.rsqrt(lax.optimization_barrier(jnp.mean(values * values, axis=-1, keepdims=True)) + norm_epsilon)

def unit_grad(pre_values, hidden_grad):
    unit_count = pre_values.shape[-1] // 2
    gate_part = pre_values[..., :unit_count]
    up_part = pre_values[..., unit_count:]
    sigma = jax.nn.sigmoid(gate_part)
    silu_value = gate_part * sigma
    silu_slope = sigma * (1.0 + gate_part * (1.0 - sigma))
    return jnp.concatenate([hidden_grad * up_part * silu_slope, hidden_grad * silu_value], axis=-1)

def norm_backward(normed_grad, rows_f32, row_scale, gain):
    scaled_grad = normed_grad * gain.astype(jnp.float32)
    rows_grad = row_scale * scaled_grad - rows_f32 * row_scale ** 3 * lax.optimization_barrier(jnp.mean(scaled_grad * rows_f32, axis=-1, keepdims=True))
    gain_grad = lax.optimization_barrier(jnp.sum(normed_grad * rows_f32 * row_scale, axis=0))
    return (gain_grad, rows_grad)

def rope_tables(length, head_width):
    positions = jnp.arange(length, dtype=jnp.float32)
    frequency = jnp.exp(-math.log(1000000.0) * jnp.arange(head_width // 2, dtype=jnp.float32) * 2.0 / head_width)
    angles = positions[:, None] * frequency[None, :]
    return (jnp.cos(angles)[:, None, :], jnp.sin(angles)[:, None, :])

def rotate(values, cosines, sines, direction):
    half_width = values.shape[-1] // 2
    front_half = values[..., :half_width]
    back_half = values[..., half_width:]
    return jnp.concatenate([front_half * cosines - direction * back_half * sines, back_half * cosines + direction * front_half * sines], axis=-1)

def masked_scores(query_part, first_row, keys_bf, segment_row, score_scale):
    row_count = query_part.shape[0]
    scores = mix('qhd,khd->hqk', query_part, keys_bf) * score_scale
    query_pos = first_row + jnp.arange(row_count, dtype=jnp.int32)
    key_pos = jnp.arange(keys_bf.shape[0], dtype=jnp.int32)
    query_seg = lax.dynamic_slice_in_dim(segment_row, first_row, row_count, 0)
    allowed = (key_pos[None, :] <= query_pos[:, None]) & (query_seg[:, None] == segment_row[None, :])
    return jnp.where(allowed[None], scores, -1e+30)

def attention_forward(queries, keys_bf, values_bf, segment_row):
    length, head_count, head_width = queries.shape
    block_rows = min(length, 512)
    score_scale = head_width ** (-0.5)

    def one_block(block_index):
        first_row = block_index * block_rows
        query_part = lax.dynamic_slice_in_dim(queries, first_row, block_rows, 0)
        scores = masked_scores(query_part, first_row, keys_bf, segment_row, score_scale)
        highest = lax.optimization_barrier(jnp.max(scores, axis=-1, keepdims=True))
        log_total = highest + jnp.log(lax.optimization_barrier(jnp.sum(jnp.exp(scores - highest), axis=-1, keepdims=True)))
        probs = jnp.exp(scores - log_total).astype(jnp.bfloat16)
        attended = mix('hqk,khd->qhd', probs, values_bf).astype(jnp.bfloat16)
        return (attended, log_total[..., 0])
    attended, log_totals = lax.map(one_block, jnp.arange(length // block_rows, dtype=jnp.int32))
    return (attended.reshape(length, head_count, head_width), log_totals)

def attention_backward(queries, keys_bf, values_bf, attended, log_totals, attended_grad, segment_row):
    length, head_count, head_width = queries.shape
    block_rows = min(length, 512)
    score_scale = head_width ** (-0.5)
    offsets = lax.optimization_barrier(jnp.sum(attended_grad.astype(jnp.float32) * attended.astype(jnp.float32), axis=-1))

    def one_block(carried, block_index):
        key_grad, value_grad = carried
        first_row = block_index * block_rows
        query_part = lax.dynamic_slice_in_dim(queries, first_row, block_rows, 0)
        grad_part = lax.dynamic_slice_in_dim(attended_grad, first_row, block_rows, 0)
        offset_part = lax.dynamic_slice_in_dim(offsets, first_row, block_rows, 0)
        scores = masked_scores(query_part, first_row, keys_bf, segment_row, score_scale)
        probs = jnp.exp(scores - log_totals[block_index][:, :, None])
        value_grad = value_grad + mix('hqk,qhd->khd', probs.astype(jnp.bfloat16), grad_part)
        prob_grad = mix('qhd,khd->hqk', grad_part, values_bf)
        score_grad = (probs * (prob_grad - jnp.transpose(offset_part)[:, :, None]) * score_scale).astype(jnp.bfloat16)
        query_grad = mix('hqk,khd->qhd', score_grad, keys_bf)
        key_grad = key_grad + mix('hqk,qhd->khd', score_grad, query_part)
        return ((key_grad, value_grad), query_grad)
    zeros_grad = jnp.zeros((length, head_count, head_width), jnp.float32)
    (key_grad, value_grad), query_grad = lax.scan(one_block, (zeros_grad, zeros_grad), jnp.arange(length // block_rows, dtype=jnp.int32))
    return (query_grad.reshape(length, head_count, head_width), key_grad, value_grad)

def capacity_positions(picks, expert_count, capacity):
    flat_picks = picks.reshape(-1).astype(jnp.int32)
    onehot = (flat_picks[:, None] == jnp.arange(expert_count, dtype=jnp.int32)[None, :]).astype(jnp.int32)
    earlier = (jnp.cumsum(onehot, axis=0) - onehot).astype(jnp.int32)
    slot_index = lax.optimization_barrier(jnp.sum(earlier * onehot, axis=1)).astype(jnp.int32)
    return flat_picks * capacity + slot_index

def slot_owners(positions, expert_count, capacity):
    pick_count = positions.shape[0]
    owners = jnp.full((expert_count * capacity,), pick_count, jnp.int32)
    return owners.at[positions].set(jnp.arange(pick_count, dtype=jnp.int32))

def attend_row(input_row, segment_row, attn_gain, qkv_weight, qkv_bias, out_weight):
    length, model_width = input_row.shape
    head_count, head_width = (qkv_weight.shape[2], qkv_weight.shape[3])
    input_f32 = input_row.astype(jnp.float32)
    scale_one = rms_scale(input_f32)
    normed_one = (input_f32 * scale_one * attn_gain.astype(jnp.float32)).astype(jnp.bfloat16)
    projected = jnp.dot(normed_one, qkv_weight.reshape(model_width, -1), preferred_element_type=jnp.float32)
    projected = projected.reshape(length, 3, head_count, head_width) + qkv_bias.astype(jnp.float32)
    cosines, sines = rope_tables(length, head_width)
    queries = rotate(projected[:, 0], cosines, sines, 1.0).astype(jnp.bfloat16)
    keys_bf = rotate(projected[:, 1], cosines, sines, 1.0).astype(jnp.bfloat16)
    values_bf = projected[:, 2].astype(jnp.bfloat16)
    attended, log_totals = attention_forward(queries, keys_bf, values_bf, segment_row)
    attn_terms = jnp.dot(attended.reshape(length, -1), out_weight.reshape(-1, model_width), preferred_element_type=jnp.float32)
    return (input_f32, scale_one, normed_one, queries, keys_bf, values_bf, attended, log_totals, attn_terms)

def reference(block_input, attn_gain, qkv_weight, qkv_bias, out_weight, ffn_gain, shared_in, shared_out, shared_gate, expert_in, expert_out, expert_picks, expert_gates, segment_ids, output_grad):
    f32 = jnp.float32
    bf16 = jnp.bfloat16
    input_rows = block_input.reshape(N_DP, LEN, D)
    grad_rows = output_grad.reshape(N_DP, LEN, D)
    unit_local = EXPERT_UNITS // N_TENSOR

    def forward_row(packed):
        pieces = attend_row(packed[0], packed[1], attn_gain, qkv_weight, qkv_bias, out_weight)
        return pieces[0] + pieces[-1]
    middle_all = lax.map(forward_row, (input_rows, segment_ids))
    middle_f32 = lax.optimization_barrier(middle_all.astype(bf16)).astype(f32)
    scale_two = rms_scale(middle_f32)
    normed_two = (middle_f32 * scale_two * ffn_gain.astype(f32)).astype(bf16)
    positions = jax.vmap(lambda picks: capacity_positions(picks, EXPERTS, CAP))(expert_picks.reshape(N_DP, LEN, TOPK))
    owners = jax.vmap(lambda placed: slot_owners(placed, EXPERTS, CAP))(positions)
    valid_slots = owners < LEN * TOPK
    row_base = jnp.arange(N_DP, dtype=jnp.int32)[:, None] * LEN
    token_ids = row_base + jnp.minimum(owners // TOPK, LEN - 1)
    pick_ids = row_base * TOPK + jnp.minimum(owners, LEN * TOPK - 1)
    slot_gates = jnp.where(valid_slots, expert_gates.reshape(-1)[pick_ids], 0.0)

    def by_expert(table):
        return jnp.swapaxes(table.reshape(N_DP, EXPERTS, CAP), 0, 1)
    normed_flat = normed_two.reshape(-1, D)
    grad_flat = output_grad.astype(f32)

    def expert_step(carried, packed):
        terms_acc, back_acc = carried
        weights_in, weights_out, tokens_here, gates_here, valid_here = packed
        token_list = tokens_here.reshape(-1)
        gate_list = gates_here.reshape(-1)
        rows_in = jnp.where(valid_here.reshape(-1)[:, None], normed_flat[token_list], jnp.zeros((), bf16))
        cot_rows = (gate_list[:, None] * grad_flat[token_list]).astype(bf16)
        pre_values = jnp.dot(rows_in, weights_in.reshape(D, -1), preferred_element_type=f32)
        hidden = (jax.nn.silu(pre_values[:, :EXPERT_UNITS]) * pre_values[:, EXPERT_UNITS:]).astype(bf16)
        group_rows = mix('mjf,jfd->mjd', hidden.reshape(-1, N_TENSOR, unit_local), weights_out.reshape(N_TENSOR, unit_local, D)).astype(bf16)
        outputs = lax.optimization_barrier(jnp.sum(group_rows.astype(f32), axis=1))
        terms_acc = terms_acc.at[token_list].add(gate_list[:, None] * outputs)
        hidden_grad = jnp.dot(cot_rows, jnp.transpose(weights_out), preferred_element_type=f32)
        pre_grad = unit_grad(pre_values, hidden_grad).astype(bf16)
        group_back = mix('mkjf,dkjf->mjd', pre_grad.reshape(-1, 2, N_TENSOR, unit_local), weights_in.reshape(D, 2, N_TENSOR, unit_local)).astype(bf16)
        back_acc = back_acc.at[token_list].add(lax.optimization_barrier(jnp.sum(group_back.astype(f32), axis=1)))
        grad_in = jnp.dot(jnp.transpose(rows_in), pre_grad, preferred_element_type=f32).reshape(D, 2, EXPERT_UNITS)
        grad_out = jnp.dot(jnp.transpose(hidden), cot_rows, preferred_element_type=f32)
        return ((terms_acc, back_acc), (grad_in, grad_out))
    zeros_tokens = jnp.zeros((N_DP * LEN, D), f32)
    (expert_terms, expert_back), (expert_in_grad, expert_out_grad) = lax.scan(expert_step, (zeros_tokens, zeros_tokens), (expert_in, expert_out, by_expert(token_ids), by_expert(slot_gates), by_expert(valid_slots)))

    def row_step(carried, packed):
        input_row, segment_row, normed_row, middle_row, scale_row, expert_row, back_row, grad_row = packed
        input_f32, scale_one, normed_one, queries, keys_bf, values_bf, attended, log_totals, attn_terms = attend_row(input_row, segment_row, attn_gain, qkv_weight, qkv_bias, out_weight)
        middle = input_f32 + attn_terms
        shared_pre = jnp.dot(normed_row, shared_in.reshape(D, -1), preferred_element_type=f32)
        shared_hidden = (jax.nn.silu(shared_pre[:, :SHARED_UNITS]) * shared_pre[:, SHARED_UNITS:]).astype(bf16)
        shared_terms = jnp.dot(shared_hidden, shared_out, preferred_element_type=f32)
        shared_weight = jax.nn.sigmoid(jnp.dot(normed_row, shared_gate, preferred_element_type=f32))
        output_row = (middle + shared_weight[:, None] * shared_terms + expert_row).astype(bf16)
        grad_f32 = grad_row.astype(f32)
        shared_cot = (shared_weight[:, None] * grad_f32).astype(bf16)
        hidden_grad = jnp.dot(shared_cot, jnp.transpose(shared_out), preferred_element_type=f32)
        shared_pre_grad = unit_grad(shared_pre, hidden_grad).astype(bf16)
        grad_shared_out = jnp.dot(jnp.transpose(shared_hidden), shared_cot, preferred_element_type=f32)
        grad_shared_in = jnp.dot(jnp.transpose(normed_row), shared_pre_grad, preferred_element_type=f32).reshape(D, 2, SHARED_UNITS)
        logit_grad = lax.optimization_barrier(jnp.sum(grad_f32 * shared_terms, axis=1)) * shared_weight * (1.0 - shared_weight)
        grad_gate = lax.optimization_barrier(jnp.sum(logit_grad[:, None] * normed_row.astype(f32), axis=0))
        normed_grad = jnp.dot(shared_pre_grad, jnp.transpose(shared_in.reshape(D, -1)), preferred_element_type=f32) + back_row + logit_grad[:, None] * shared_gate.astype(f32)
        grad_gain_two, middle_grad = norm_backward(normed_grad, middle_row, scale_row, ffn_gain)
        middle_grad = middle_grad + grad_f32
        attn_cot = middle_grad.astype(bf16)
        grad_out_weight = jnp.dot(jnp.transpose(attended.reshape(LEN, -1)), attn_cot, preferred_element_type=f32).reshape(HEADS, HEAD_DIM, D)
        attended_grad = jnp.dot(attn_cot, jnp.transpose(out_weight.reshape(-1, D)), preferred_element_type=f32).reshape(LEN, HEADS, HEAD_DIM).astype(bf16)
        query_grad, key_grad, value_grad = attention_backward(queries, keys_bf, values_bf, attended, log_totals, attended_grad, segment_row)
        cosines, sines = rope_tables(LEN, HEAD_DIM)
        projected_grad = jnp.stack([rotate(query_grad, cosines, sines, -1.0), rotate(key_grad, cosines, sines, -1.0), value_grad], axis=1)
        grad_bias = lax.optimization_barrier(jnp.sum(projected_grad, axis=0))
        projected_cot = projected_grad.reshape(LEN, -1).astype(bf16)
        grad_qkv = jnp.dot(jnp.transpose(normed_one), projected_cot, preferred_element_type=f32).reshape(D, 3, HEADS, HEAD_DIM)
        normed_one_grad = jnp.dot(projected_cot, jnp.transpose(qkv_weight.reshape(D, -1)), preferred_element_type=f32)
        grad_gain_one, input_grad = norm_backward(normed_one_grad, input_f32, scale_one, attn_gain)
        input_grad = input_grad + middle_grad
        updates = (grad_gain_one, grad_qkv, grad_bias, grad_out_weight, grad_gain_two, grad_shared_in, grad_shared_out, grad_gate)
        carried = tuple((total + piece for total, piece in zip(carried, updates)))
        return (carried, (output_row, input_grad))
    start_grads = (jnp.zeros((D,), f32), jnp.zeros((D, 3, HEADS, HEAD_DIM), f32), jnp.zeros((3, HEADS, HEAD_DIM), f32), jnp.zeros((HEADS, HEAD_DIM, D), f32), jnp.zeros((D,), f32), jnp.zeros((D, 2, SHARED_UNITS), f32), jnp.zeros((SHARED_UNITS, D), f32), jnp.zeros((D,), f32))
    packed_rows = (input_rows, segment_ids, normed_two, middle_f32, scale_two, expert_terms.reshape(N_DP, LEN, D), expert_back.reshape(N_DP, LEN, D), grad_rows)
    final_grads, (output_rows, input_grads) = lax.scan(row_step, start_grads, packed_rows)
    return (output_rows.reshape(-1, D), input_grads.reshape(-1, D), final_grads[0], final_grads[1], final_grads[2], final_grads[3], final_grads[4], final_grads[5], final_grads[6], final_grads[7], expert_in_grad, expert_out_grad)
```

```python
import math

import jax
import jax.numpy as jnp
from jax import lax
from jax.sharding import PartitionSpec as P


norm_epsilon = 1e-06
f32 = jnp.float32
bf16 = jnp.bfloat16
lanes = 128
aux_rows = 8
gathered_limit = 1 << 25


def dot(left, right, left_dim, right_dim, out=f32):
    return lax.dot_general(
        left, right, (((left_dim,), (right_dim,)), ((), ())), preferred_element_type=f32
    ).astype(out)


def batched(left, right, left_dim, right_dim, out=f32):
    return lax.dot_general(
        left, right, (((left_dim,), (right_dim,)), ((0,), (0,))), preferred_element_type=f32
    ).astype(out)


def rms_scale(values):
    return lax.rsqrt(jnp.mean(values * values, axis=-1, keepdims=True) + norm_epsilon)


def unit_slopes(gate_part):
    sigma = jax.nn.sigmoid(gate_part)
    return gate_part * sigma, sigma * (1.0 + gate_part * (1.0 - sigma))


def rotate(values, cosines, sines, direction):
    half_width = values.shape[-1] // 2
    front_half = values[..., :half_width]
    back_half = values[..., half_width:]
    return jnp.concatenate(
        [
            front_half * cosines - direction * back_half * sines,
            back_half * cosines + direction * front_half * sines,
        ],
        axis=-1,
    )


def pick(stack, index):
    return lax.dynamic_index_in_dim(stack, index, 0, keepdims=False)


def place(buffer, block, index):
    return lax.dynamic_update_index_in_dim(buffer, block, index, 0)


class Links:
    def __init__(self):
        self.count = lax.axis_size("dp")
        self.corners = 4
        self.levels = self.count // self.corners
        index = lax.axis_index("dp")
        self.index = index
        self.corner = index % self.corners
        self.level = index // self.corners
        self.half = lax.axis_index("tensor")

    def flip(self, block, bits):
        return lax.ppermute(block, "dp", [(i, i ^ bits) for i in range(self.count)])

    def lift(self, block):
        return lax.ppermute(
            block, "dp", [(i, (i + self.corners) % self.count) for i in range(self.count)]
        )

    def swap(self, block):
        return lax.ppermute(block, "tensor", [(0, 1), (1, 0)])

    def from_level(self, step):
        return (self.level + self.levels - step) % self.levels

    def plane_gather(self, block, order):
        first, second = (1, 2) if order == 0 else (2, 1)
        one = self.flip(block, first)
        two = self.flip(block, second)
        both = self.flip(one, second)
        return [block, one, two, both] if order == 0 else [block, two, one, both]

    def plane_rows(self, block, order):
        mine = self.plane_gather(block, order)
        theirs = [self.swap(piece) for piece in mine]
        return jnp.stack([jnp.stack(pair) for pair in zip(mine, theirs)])

    def plane_reduce(self, rows, order):
        other = self.swap(rows[:, 1])
        total = rows[:, 0].astype(f32) + other.astype(f32)
        parts = total.astype(bf16)
        first, second = (1, 2) if order == 0 else (2, 1)
        through = self.flip(parts[3], second)
        joined = (parts[first].astype(f32) + through.astype(f32)).astype(bf16)
        near = self.flip(joined, first)
        side = self.flip(parts[second], second)
        return parts[0].astype(f32) + near.astype(f32) + side.astype(f32)

    def spread_small(self, block):
        held = block[None]
        bits = 1
        while bits < self.count:
            held = jnp.concatenate([held, self.flip(held, bits)], axis=0)
            bits *= 2
        return held


def attention_tables(half, length, head_width):
    own = length // 2
    spots = jnp.arange(own, dtype=jnp.int32)
    positions = jnp.concatenate([half * own + spots, (1 - half) * own + spots])
    frequency = jnp.exp(
        -math.log(1000000.0) * jnp.arange(head_width // 2, dtype=f32) * 2.0 / head_width
    )
    angles = positions.astype(f32)[:, None] * frequency[None, :]
    return positions, jnp.cos(angles)[None], jnp.sin(angles)[None]


def routed(members, capacity):
    token_count = members.shape[1]
    upto = (
        jnp.arange(token_count, dtype=jnp.int32)[:, None]
        < jnp.arange(token_count, dtype=jnp.int32)[None, :]
    ).astype(bf16)
    slot = dot(members.astype(bf16), upto, 1, 0)
    places = jnp.arange(capacity, dtype=jnp.int32).astype(f32)
    return ((slot[:, None, :] == places[None, :, None]) & (members[:, None, :] > 0)).astype(bf16)


def body(
    block_input,
    attn_gain,
    qkv_weight,
    qkv_bias,
    out_weight,
    ffn_gain,
    shared_in,
    shared_out,
    shared_gate,
    expert_in,
    expert_out,
    expert_picks,
    expert_gates,
    segment_ids,
    output_grad,
):
    links = Links()
    count, corners, levels = links.count, links.corners, links.levels
    own_count, width = block_input.shape
    length, top_count = expert_picks.shape
    block = attn_gain.shape[0]
    local_experts = expert_in.shape[0]
    expert_count = local_experts * count
    capacity = length * top_count * 3 // (2 * expert_count)
    head_width = qkv_weight.shape[3]
    three = 3 * head_width
    wide = 4 * head_width
    tokens = corners * length
    score_scale = head_width ** (-0.5)

    table = jnp.concatenate(
        [expert_picks.astype(f32).T, expert_gates.T], axis=0
    )
    tables = links.spread_small(table)
    grad_all = lax.all_gather(output_grad, ("dp", "tensor"), axis=0, tiled=True).reshape(
        levels, corners, 2, own_count, width
    )

    unit_count = shared_out.shape[0] // count
    in_turned = jnp.transpose(shared_in, (1, 2, 0)).reshape(2, count, unit_count, block)
    shared_sent = jnp.concatenate(
        [in_turned[0], in_turned[1], shared_out.reshape(count, unit_count, block)], axis=1
    )
    shared_here = lax.all_to_all(shared_sent, "dp", split_axis=0, concat_axis=0, tiled=True)
    shared_here = jnp.transpose(shared_here, (1, 0, 2)).reshape(3 * unit_count, width)

    gain_one = attn_gain.astype(f32)
    scaled_qkv = (qkv_weight.astype(f32) * gain_one[:, None, None, None]).astype(bf16)
    head_block = jnp.concatenate(
        [
            jnp.transpose(scaled_qkv, (2, 0, 1, 3)).reshape(corners, block, three),
            jnp.transpose(out_weight, (0, 2, 1)),
        ],
        axis=2,
    )
    part = head_width // count
    aux = jnp.zeros((corners, aux_rows, wide), bf16)
    aux = aux.at[:, 0, :block].set(ffn_gain[None])
    aux = aux.at[:, 0, block : 2 * block].set(shared_gate[None])
    aux = aux.at[:, 0, 2 * block : 2 * block + 3 * part].set(
        jnp.transpose(qkv_bias, (1, 0, 2)).reshape(corners, 3 * part)
    )
    aux = aux.at[:, 1, :length].set(segment_ids.astype(bf16))
    payload = jnp.concatenate([head_block, aux], axis=1)
    plane_blocks = [pick(payload, links.corner)]
    for k in range(1, corners):
        plane_blocks.append(links.flip(pick(payload, links.corner ^ k), k))
    segments = jnp.stack([piece[block + 1, :length] for piece in plane_blocks])
    plane_weights = jnp.zeros((corners, block + aux_rows, wide), bf16)
    for k in range(corners):
        plane_weights = place(plane_weights, plane_blocks[k], links.corner ^ k)
    all_weights = jnp.zeros((levels, corners, block + aux_rows, wide), bf16)
    passing = plane_weights
    for k in range(levels):
        all_weights = place(all_weights, passing, links.from_level(k))
        if k + 1 < levels:
            passing = links.lift(passing)
    weights = all_weights[:, :, :block].reshape(width, wide)
    extras = all_weights[:, :, block].reshape(count, wide)
    gain_two = extras[:, :block].reshape(width).astype(f32)
    gate_row = extras[:, block : 2 * block].reshape(1, width)
    bias = jnp.transpose(
        extras[:, 2 * block : 2 * block + 3 * part].reshape(count, 3, part), (1, 0, 2)
    ).reshape(1, three)

    input_f32 = block_input.astype(f32)
    scale_one = rms_scale(input_f32)
    scaled_input = (input_f32 * scale_one).astype(bf16)
    rows_one = links.plane_rows(scaled_input, 0).reshape(tokens, width)
    qkv_part, out_part = weights[:, :three], weights[:, three:]
    projected = dot(rows_one, qkv_part, 1, 0) + bias.astype(f32)
    projected = projected.reshape(corners, length, three)
    positions, cosines, sines = attention_tables(links.half, length, head_width)
    queries = rotate(projected[..., :head_width], cosines, sines, 1.0).astype(bf16)
    keys = rotate(projected[..., head_width : 2 * head_width], cosines, sines, 1.0).astype(bf16)
    values = projected[..., 2 * head_width :].astype(bf16)
    segments = jnp.where(links.half == 0, segments, jnp.roll(segments, own_count, axis=1))
    allowed = (positions[None, None, :] <= positions[None, :, None]) & (
        segments[:, :, None] == segments[:, None, :]
    )
    scores = jnp.where(allowed, batched(queries, keys, 2, 2) * score_scale, -1e30)
    highest = jnp.max(scores, axis=-1, keepdims=True)
    log_totals = highest + jnp.log(jnp.sum(jnp.exp(scores - highest), axis=-1, keepdims=True))
    probs = jnp.exp(scores - log_totals).astype(bf16)
    attended = batched(probs, values, 2, 1, bf16)
    attn_terms = dot(attended.reshape(tokens, head_width), out_part, 1, 1, bf16)
    middle = input_f32 + links.plane_reduce(
        attn_terms.reshape(corners, 2, own_count, width), 0
    )

    middle_f32 = middle.astype(bf16).astype(f32)
    scale_two = rms_scale(middle_f32)
    normed_two = (middle_f32 * scale_two * gain_two[None]).astype(bf16)

    padded = -(-(unit_count + 1) // lanes) * lanes
    gap = jnp.zeros((padded - unit_count, width), bf16)
    shared_pair = jnp.concatenate(
        [
            shared_here[:unit_count],
            gap,
            shared_here[unit_count : 2 * unit_count],
            gate_row,
            gap[1:],
        ],
        axis=0,
    )
    shared_down = jnp.concatenate([shared_here[2 * unit_count :], gap], axis=0)
    is_gate = jnp.arange(padded, dtype=jnp.int32)[None, :] == unit_count
    unit_local = expert_out.shape[1]
    in_flat = expert_in.reshape(local_experts, width, 2 * unit_local)
    first_expert = (links.index * local_experts).astype(f32)

    def level_work(rows_two, step):
        origin = links.from_level(step)
        level_grads = pick(grad_all, origin)
        grad_rows = jnp.stack(
            [
                jnp.stack(
                    [
                        pick(pick(level_grads, links.corner ^ j), links.half),
                        pick(pick(level_grads, links.corner ^ j), 1 - links.half),
                    ]
                )
                for j in range(corners)
            ]
        ).reshape(corners, length, width)
        here = jnp.stack(
            [
                pick(tables, (origin * corners + (links.corner ^ j)) ^ links.index)
                for j in range(corners)
            ]
        )
        here = jnp.where(links.half == 0, here, jnp.roll(here, own_count, axis=2))
        flat_rows = rows_two.reshape(tokens, width)
        flat_grads = grad_rows.reshape(tokens, width)
        pre = dot(flat_rows, shared_pair, 1, 1)
        silu_value, silu_slope = unit_slopes(pre[:, :padded])
        up_part = pre[:, padded:]
        weight = jax.nn.sigmoid(
            jnp.sum(jnp.where(is_gate, up_part, 0.0), axis=1, keepdims=True)
        )
        hidden = silu_value * up_part
        raw_grad = dot(flat_grads, shared_down, 1, 1)
        logit_grad = (
            jnp.sum(raw_grad * hidden, axis=1, keepdims=True) * weight * (1.0 - weight)
        )
        hidden_grad = raw_grad * weight
        shared_pre_grad = jnp.concatenate(
            [
                hidden_grad * up_part * silu_slope,
                jnp.where(is_gate, logit_grad, hidden_grad * silu_value),
            ],
            axis=1,
        ).astype(bf16)
        weighted_hidden = (hidden * weight).astype(bf16)
        terms = dot(weighted_hidden, shared_down, 1, 0)
        backs = dot(shared_pre_grad, shared_pair, 1, 0)
        shared_grads = (
            dot(shared_pre_grad, flat_rows, 0, 0),
            dot(weighted_hidden, flat_grads, 0, 0),
        )
        kept = []
        for x in range(local_experts):
            chosen = here[:, :top_count] == first_expert + x
            members = jnp.sum(chosen.astype(f32), axis=1)
            token_gates = jnp.sum(jnp.where(chosen, here[:, top_count:], 0.0), axis=1)
            onehot = routed(members, capacity)
            slot_gates = jnp.sum(
                onehot.astype(f32) * token_gates[:, None, :], axis=2
            ).reshape(corners * capacity, 1)
            rows_in = batched(onehot, rows_two, 2, 1, bf16).reshape(-1, width)
            cots_in = batched(onehot, grad_rows, 2, 1, bf16).reshape(-1, width)
            expert_pre = dot(rows_in, in_flat[x], 1, 0)
            expert_silu, expert_slope = unit_slopes(expert_pre[:, :unit_local])
            expert_up = expert_pre[:, unit_local:]
            expert_hidden = (slot_gates * (expert_silu * expert_up)).astype(bf16)
            expert_grad = slot_gates * dot(cots_in, expert_out[x], 1, 1)
            expert_pre_grad = jnp.concatenate(
                [expert_grad * expert_up * expert_slope, expert_grad * expert_silu], axis=1
            ).astype(bf16)
            out_rows = dot(expert_hidden, expert_out[x], 1, 0, bf16)
            back_rows = dot(expert_pre_grad, in_flat[x], 1, 1, bf16)
            terms = terms + batched(
                onehot, out_rows.reshape(corners, capacity, width), 1, 1
            ).reshape(tokens, width)
            backs = backs + batched(
                onehot, back_rows.reshape(corners, capacity, width), 1, 1
            ).reshape(tokens, width)
            kept.append((rows_in, cots_in, expert_hidden, expert_pre_grad))
        shape = (corners, 2, own_count, width)
        return terms.astype(bf16).reshape(shape), backs.astype(bf16).reshape(shape), shared_grads, kept

    passing = normed_two
    results = []
    for k in range(levels):
        rows_two = links.plane_rows(passing, k % 2).reshape(corners, length, width)
        if k + 1 < levels:
            passing = links.lift(passing)
        results.append(level_work(rows_two, k))

    def level_reduce(which):
        total = None
        for k in list(range(1, levels)) + [0]:
            here = links.plane_reduce(results[k][which], k % 2)
            total = here if total is None else total.astype(f32) + here
            if k:
                total = links.lift(total.astype(bf16))
        return total

    normed_grad = level_reduce(1)

    grad_f32 = output_grad.astype(f32)
    scaled_grad = normed_grad * gain_two[None]
    middle_grad = (
        grad_f32
        + scale_two * scaled_grad
        - middle_f32 * scale_two**3 * jnp.mean(scaled_grad * middle_f32, axis=-1, keepdims=True)
    )
    gain_two_part = jnp.sum(normed_grad * middle_f32 * scale_two, axis=0)
    attn_cot = middle_grad.astype(bf16)
    cot_rows = links.plane_rows(attn_cot, 1).reshape(tokens, width)
    attended_grad = dot(cot_rows, out_part, 1, 0, bf16).reshape(corners, length, head_width)
    offsets = jnp.sum(
        attended_grad.astype(f32) * attended.astype(f32), axis=-1, keepdims=True
    )
    exact = jnp.exp(scores - log_totals)
    value_grad = batched(exact.astype(bf16), attended_grad, 1, 1)
    prob_grad = batched(attended_grad, values, 2, 2)
    score_grad = (exact * (prob_grad - offsets) * score_scale).astype(bf16)
    query_grad = rotate(batched(score_grad, keys, 2, 1), cosines, sines, -1.0)
    key_grad = rotate(batched(score_grad, queries, 1, 1), cosines, sines, -1.0)
    projected_grad = jnp.concatenate([query_grad, key_grad, value_grad], axis=-1).reshape(
        tokens, three
    )
    bias_part = jnp.sum(projected_grad, axis=0)
    projected_cot = projected_grad.astype(bf16)
    scaled_part = dot(projected_cot, qkv_part, 1, 1, bf16)
    scaled_grad_one = links.plane_reduce(scaled_part.reshape(corners, 2, own_count, width), 1)
    head_grads = jnp.concatenate(
        [
            dot(rows_one, projected_cot, 0, 0, bf16),
            dot(cot_rows, attended.reshape(tokens, head_width), 0, 0, bf16),
        ],
        axis=1,
    ).reshape(count, block, wide)
    aux_grads = jnp.zeros((count, aux_rows, wide), bf16)
    aux_grads = aux_grads.at[:, 0, :block].set(gain_two_part.astype(bf16).reshape(count, block))
    aux_grads = aux_grads.at[:, 0, block : block + 3 * part].set(
        jnp.transpose(bias_part.astype(bf16).reshape(3, count, part), (1, 0, 2)).reshape(
            count, 3 * part
        )
    )
    sent_grads = jnp.concatenate([head_grads, aux_grads], axis=1).reshape(
        levels, corners, block + aux_rows, wide
    )
    total = None
    for k in list(range(1, levels)) + [0]:
        here = pick(sent_grads, links.from_level(k))
        total = here if total is None else (total.astype(f32) + here.astype(f32)).astype(bf16)
        if k:
            total = links.lift(total)
    heads_here = jnp.zeros((corners, block + aux_rows, wide), bf16)
    for k in range(corners):
        piece = pick(total, links.corner ^ k)
        if k:
            piece = links.flip(piece, k)
        heads_here = place(heads_here, piece, links.corner ^ k)
    heads_f32 = heads_here.astype(f32)
    raw_qkv = jnp.transpose(
        heads_f32[:, :block, :three].reshape(corners, block, 3, head_width), (1, 2, 0, 3)
    )
    grad_qkv = raw_qkv * gain_one[:, None, None, None]
    gain_one_part = jnp.sum(raw_qkv * qkv_weight.astype(f32), axis=(1, 2, 3))
    grad_out_weight = jnp.transpose(heads_f32[:, :block, three:], (0, 2, 1))
    grad_bias = jnp.transpose(
        heads_f32[:, block, block : block + 3 * part].reshape(corners, 3, part), (1, 0, 2)
    )
    gain_two_sum = jnp.sum(heads_f32[:, block, :block], axis=0)

    input_grad = (
        middle_grad
        + scale_one * scaled_grad_one
        - input_f32
        * scale_one**3
        * jnp.mean(scaled_grad_one * input_f32, axis=-1, keepdims=True)
    )
    block_output = (middle + level_reduce(0)).astype(bf16)

    pair_grad = sum(result[2][0] for result in results)
    down_grad = sum(result[2][1] for result in results)
    shared_back = jnp.concatenate(
        [
            pair_grad[:unit_count],
            pair_grad[padded : padded + unit_count],
            down_grad[:unit_count],
            pair_grad[padded + unit_count : padded + unit_count + 1],
        ],
        axis=0,
    ).astype(bf16)
    shared_back = jnp.transpose(
        shared_back.reshape(3 * unit_count + 1, count, block), (1, 0, 2)
    )
    shared_home = lax.all_to_all(shared_back, "dp", split_axis=0, concat_axis=0, tiled=True)
    home = shared_home[:, : 2 * unit_count].astype(f32).reshape(count, 2, unit_count, block)
    grad_shared_in = jnp.transpose(home, (3, 1, 0, 2)).reshape(shared_in.shape)
    grad_shared_out = (
        shared_home[:, 2 * unit_count : 3 * unit_count].astype(f32).reshape(shared_out.shape)
    )
    gate_part = jnp.sum(shared_home[:, 3 * unit_count].astype(f32), axis=0)
    in_grads, out_grads = [], []
    for x in range(local_experts):
        gathered = [
            jnp.concatenate([result[3][x][n] for result in results], axis=0) for n in range(4)
        ]
        in_grads.append(dot(gathered[0], gathered[3], 0, 0))
        out_grads.append(dot(gathered[2], gathered[1], 0, 0))
    expert_in_grad = jnp.stack(in_grads).reshape(expert_in.shape)
    expert_out_grad = jnp.stack(out_grads)

    vectors = jnp.stack([gain_one_part, gain_two_sum, gate_part])
    vectors = vectors + links.swap(vectors)
    return (
        block_output,
        input_grad,
        vectors[0],
        grad_qkv,
        grad_bias,
        grad_out_weight,
        vectors[1],
        grad_shared_in,
        grad_shared_out,
        vectors[2],
        expert_in_grad,
        expert_out_grad,
    )


def mix(form, left, right):
    return jnp.einsum(form, left, right, preferred_element_type=jnp.float32)


def unit_grad(pre_values, hidden_grad):
    unit_count = pre_values.shape[-1] // 2
    gate_part = pre_values[..., :unit_count]
    up_part = pre_values[..., unit_count:]
    sigma = jax.nn.sigmoid(gate_part)
    silu_value = gate_part * sigma
    silu_slope = sigma * (1.0 + gate_part * (1.0 - sigma))
    return jnp.concatenate([hidden_grad * up_part * silu_slope, hidden_grad * silu_value], axis=-1)


def norm_backward(normed_grad, rows_f32, row_scale, gain):
    scaled_grad = normed_grad * gain.astype(jnp.float32)
    rows_grad = row_scale * scaled_grad - rows_f32 * row_scale**3 * jnp.mean(
        scaled_grad * rows_f32, axis=-1, keepdims=True
    )
    gain_grad = jnp.sum(normed_grad * rows_f32 * row_scale, axis=0)
    return (gain_grad, rows_grad)


def rope_tables(length, head_width):
    positions = jnp.arange(length, dtype=jnp.float32)
    frequency = jnp.exp(
        -math.log(1000000.0) * jnp.arange(head_width // 2, dtype=jnp.float32) * 2.0 / head_width
    )
    angles = positions[:, None] * frequency[None, :]
    return (jnp.cos(angles)[:, None, :], jnp.sin(angles)[:, None, :])


def masked_scores(query_part, first_row, keys_bf, segment_row, score_scale):
    row_count = query_part.shape[0]
    scores = mix("qhd,khd->hqk", query_part, keys_bf) * score_scale
    query_pos = first_row + jnp.arange(row_count, dtype=jnp.int32)
    key_pos = jnp.arange(keys_bf.shape[0], dtype=jnp.int32)
    allowed = (key_pos[None, :] <= query_pos[:, None]) & (
        segment_row[:, None] == segment_row[None, :]
    )
    return jnp.where(allowed[None], scores, -1e30)


def attention_forward(queries, keys_bf, values_bf, segment_row):
    length, head_count, head_width = queries.shape
    block_rows = min(length, 512)
    score_scale = head_width ** (-0.5)

    def one_block(block_index):
        first_row = block_index * block_rows
        scores = masked_scores(queries, first_row, keys_bf, segment_row, score_scale)
        highest = jnp.max(scores, axis=-1, keepdims=True)
        log_total = highest + jnp.log(jnp.sum(jnp.exp(scores - highest), axis=-1, keepdims=True))
        probs = jnp.exp(scores - log_total).astype(jnp.bfloat16)
        attended = mix("hqk,khd->qhd", probs, values_bf).astype(jnp.bfloat16)
        return (attended, log_total[..., 0])

    attended, log_totals = lax.map(one_block, jnp.arange(length // block_rows, dtype=jnp.int32))
    return (attended.reshape(length, head_count, head_width), log_totals)


def attention_backward(
    queries, keys_bf, values_bf, attended, log_totals, attended_grad, segment_row
):
    length, head_count, head_width = queries.shape
    block_rows = min(length, 512)
    score_scale = head_width ** (-0.5)
    offsets = jnp.sum(attended_grad.astype(jnp.float32) * attended.astype(jnp.float32), axis=-1)

    def one_block(carried, block_index):
        key_grad, value_grad = carried
        first_row = block_index * block_rows
        scores = masked_scores(queries, first_row, keys_bf, segment_row, score_scale)
        probs = jnp.exp(scores - log_totals[block_index][:, :, None])
        value_grad = value_grad + mix("hqk,qhd->khd", probs.astype(jnp.bfloat16), attended_grad)
        prob_grad = mix("qhd,khd->hqk", attended_grad, values_bf)
        score_grad = (
            probs * (prob_grad - jnp.transpose(offsets)[:, :, None]) * score_scale
        ).astype(jnp.bfloat16)
        query_grad = mix("hqk,khd->qhd", score_grad, keys_bf)
        key_grad = key_grad + mix("hqk,qhd->khd", score_grad, queries)
        return ((key_grad, value_grad), query_grad)

    zeros_grad = jnp.zeros((length, head_count, head_width), jnp.float32)
    (key_grad, value_grad), query_grad = lax.scan(
        one_block, (zeros_grad, zeros_grad), jnp.arange(length // block_rows, dtype=jnp.int32)
    )
    return (query_grad.reshape(length, head_count, head_width), key_grad, value_grad)


def capacity_positions(picks, expert_count, capacity):
    flat_picks = picks.reshape(-1)
    onehot = (flat_picks[:, None] == jnp.arange(expert_count, dtype=jnp.int32)[None, :]).astype(
        jnp.int32
    )
    earlier = jnp.cumsum(onehot, axis=0) - onehot
    slot_index = jnp.sum(earlier * onehot, axis=1)
    return flat_picks * capacity + slot_index


def slot_owners(positions, expert_count, capacity):
    pick_count = positions.shape[0]
    owners = jnp.full((expert_count * capacity,), pick_count, jnp.int32)
    return owners.at[positions].set(jnp.arange(pick_count, dtype=jnp.int32))


def attend_row(input_row, segment_row, attn_gain, qkv_weight, qkv_bias, out_weight):
    length, model_width = input_row.shape
    head_count, head_width = (qkv_weight.shape[2], qkv_weight.shape[3])
    input_f32 = input_row.astype(jnp.float32)
    scale_one = rms_scale(input_f32)
    normed_one = (input_f32 * scale_one * attn_gain.astype(jnp.float32)).astype(jnp.bfloat16)
    projected = jnp.dot(
        normed_one, qkv_weight.reshape(model_width, -1), preferred_element_type=jnp.float32
    )
    projected = projected.reshape(length, 3, head_count, head_width) + qkv_bias.astype(jnp.float32)
    cosines, sines = rope_tables(length, head_width)
    queries = rotate(projected[:, 0], cosines, sines, 1.0).astype(jnp.bfloat16)
    keys_bf = rotate(projected[:, 1], cosines, sines, 1.0).astype(jnp.bfloat16)
    values_bf = projected[:, 2].astype(jnp.bfloat16)
    attended, log_totals = attention_forward(queries, keys_bf, values_bf, segment_row)
    attn_terms = jnp.dot(
        attended.reshape(length, -1),
        out_weight.reshape(-1, model_width),
        preferred_element_type=jnp.float32,
    )
    return (
        input_f32,
        scale_one,
        normed_one,
        queries,
        keys_bf,
        values_bf,
        attended,
        log_totals,
        attn_terms,
    )


def spread(own_rows):
    return lax.all_gather(own_rows, "tensor", axis=0, tiled=True)


def fold(row_terms):
    return lax.psum_scatter(
        row_terms.astype(jnp.bfloat16), "tensor", scatter_dimension=0, tiled=True
    ).astype(jnp.float32)


def dispatch(slot_rows):
    return lax.all_to_all(slot_rows, "dp", split_axis=0, concat_axis=0, tiled=True)


def collect(slot_rows):
    return lax.all_to_all(slot_rows, "dp", split_axis=0, concat_axis=0, tiled=True)


def body_by_slots(
    block_input,
    attn_gain,
    qkv_weight,
    qkv_bias,
    out_weight,
    ffn_gain,
    shared_in,
    shared_out,
    shared_gate,
    expert_in,
    expert_out,
    expert_picks,
    expert_gates,
    segment_ids,
    output_grad,
):
    length, top_count = expert_picks.shape
    model_width = block_input.shape[1]
    dp_count = lax.axis_size("dp")
    local_experts = expert_in.shape[0]
    expert_count = local_experts * dp_count
    capacity = length * top_count * 3 // (2 * expert_count)
    own_count = block_input.shape[0]
    segment_row = segment_ids[0]
    gain_one, qkv_full, bias_full, out_full = (
        lax.all_gather(attn_gain, "dp", axis=0, tiled=True),
        lax.all_gather(qkv_weight, "dp", axis=0, tiled=True),
        lax.all_gather(qkv_bias, "dp", axis=2, tiled=True),
        lax.all_gather(out_weight, "dp", axis=2, tiled=True),
    )
    gain_two, shared_in_full, shared_out_full, gate_vector = (
        lax.all_gather(ffn_gain, "dp", axis=0, tiled=True),
        lax.all_gather(shared_in, "dp", axis=0, tiled=True),
        lax.all_gather(shared_out, "dp", axis=1, tiled=True),
        lax.all_gather(shared_gate, "dp", axis=0, tiled=True),
    )
    head_count, head_width = (qkv_full.shape[2], qkv_full.shape[3])
    input_rows = spread(block_input)
    (
        input_f32,
        scale_one,
        normed_one,
        queries,
        keys_bf,
        values_bf,
        attended,
        log_totals,
        attn_terms,
    ) = attend_row(input_rows, segment_row, gain_one, qkv_full, bias_full, out_full)
    middle = block_input.astype(f32) + fold(attn_terms)
    middle_rows = spread(middle.astype(bf16))
    middle_f32 = middle_rows.astype(f32)
    scale_two = rms_scale(middle_f32)
    normed_two = (middle_f32 * scale_two * gain_two.astype(f32)).astype(bf16)
    shared_in_flat = shared_in_full.reshape(model_width, -1)
    shared_pre = jnp.dot(normed_two, shared_in_flat, preferred_element_type=f32)
    shared_units = shared_pre.shape[1] // 2
    shared_hidden = (
        jax.nn.silu(shared_pre[:, :shared_units]) * shared_pre[:, shared_units:]
    ).astype(bf16)
    shared_terms = jnp.dot(shared_hidden, shared_out_full, preferred_element_type=f32)
    shared_weight = jax.nn.sigmoid(jnp.dot(normed_two, gate_vector, preferred_element_type=f32))
    positions = capacity_positions(expert_picks, expert_count, capacity)
    owners = slot_owners(positions, expert_count, capacity)
    valid_slots = owners < length * top_count
    owner_tokens = jnp.minimum(owners // top_count, length - 1)
    sent_rows = jnp.where(
        valid_slots[:, None], normed_two[owner_tokens], jnp.zeros((), bf16)
    ).reshape(expert_count, capacity, model_width)
    arrived = dispatch(sent_rows).reshape(dp_count, local_experts, capacity, model_width)
    in_flat = expert_in.reshape(local_experts, model_width, -1)
    expert_pre = mix("sxcd,xdf->sxcf", arrived, in_flat)
    unit_local = expert_pre.shape[-1] // 2
    expert_hidden = (
        jax.nn.silu(expert_pre[..., :unit_local]) * expert_pre[..., unit_local:]
    ).astype(bf16)
    expert_rows = mix("sxcf,xfd->sxcd", expert_hidden, expert_out).astype(bf16)
    returned = collect(expert_rows.reshape(-1, capacity, model_width)).reshape(-1, model_width)
    picked = returned[positions].reshape(length, top_count, model_width).astype(f32)
    expert_terms = jnp.sum(expert_gates[:, :, None] * picked, axis=1)
    ffn_out = fold(shared_weight[:, None] * shared_terms + expert_terms)
    block_output = (middle + ffn_out).astype(bf16)
    grad_rows = spread(output_grad)
    grad_f32 = grad_rows.astype(f32)
    shared_cot = (shared_weight[:, None] * grad_f32).astype(bf16)
    hidden_grad = jnp.dot(shared_cot, jnp.transpose(shared_out_full), preferred_element_type=f32)
    shared_pre_grad = unit_grad(shared_pre, hidden_grad).astype(bf16)
    grad_shared_out = jnp.dot(jnp.transpose(shared_hidden), shared_cot, preferred_element_type=f32)
    grad_shared_in = jnp.dot(
        jnp.transpose(normed_two), shared_pre_grad, preferred_element_type=f32
    ).reshape(shared_in_full.shape)
    gate_dot = jnp.sum(grad_f32 * shared_terms, axis=1)
    slot_gates = jnp.where(
        valid_slots, expert_gates.reshape(-1)[jnp.minimum(owners, length * top_count - 1)], 0.0
    )
    cot_sent = (
        (slot_gates[:, None] * grad_f32[owner_tokens])
        .astype(bf16)
        .reshape(expert_count, capacity, model_width)
    )
    cot_arrived = dispatch(cot_sent).reshape(dp_count, local_experts, capacity, model_width)
    rows_again, pre_again, hidden_again = (arrived, expert_pre, expert_hidden)
    expert_hidden_grad = mix("sxcd,xfd->sxcf", cot_arrived, expert_out)
    expert_pre_grad = unit_grad(pre_again, expert_hidden_grad).astype(bf16)
    back_rows = mix("sxcf,xdf->sxcd", expert_pre_grad, in_flat).astype(bf16)
    expert_in_grad = mix("sxcd,sxcf->xdf", rows_again, expert_pre_grad).reshape(expert_in.shape)
    expert_out_grad = mix("sxcf,sxcd->xfd", hidden_again, cot_arrived)
    back_returned = collect(back_rows.reshape(-1, capacity, model_width)).reshape(-1, model_width)
    expert_back = jnp.sum(
        back_returned[positions].reshape(length, top_count, model_width).astype(f32), axis=1
    )
    normed_part = (
        jnp.dot(shared_pre_grad, jnp.transpose(shared_in_flat), preferred_element_type=f32)
        + expert_back
    )
    normed_sum, gate_sum = (
        lax.psum(normed_part.astype(jnp.bfloat16), "tensor").astype(jnp.float32),
        lax.psum(gate_dot.astype(jnp.bfloat16), "tensor").astype(jnp.float32),
    )
    logit_grad = gate_sum * shared_weight * (1.0 - shared_weight)
    normed_grad = normed_sum + logit_grad[:, None] * gate_vector.astype(f32)
    grad_gate = jnp.sum(logit_grad[:, None] * normed_two.astype(f32), axis=0)
    grad_gain_two, middle_grad = norm_backward(normed_grad, middle_f32, scale_two, gain_two)
    middle_grad = middle_grad + grad_f32
    attn_cot = middle_grad.astype(bf16)
    grad_out_weight = jnp.dot(
        jnp.transpose(attended.reshape(length, -1)), attn_cot, preferred_element_type=f32
    ).reshape(out_full.shape)
    attended_grad = (
        jnp.dot(
            attn_cot, jnp.transpose(out_full.reshape(-1, model_width)), preferred_element_type=f32
        )
        .reshape(length, head_count, head_width)
        .astype(bf16)
    )
    query_grad, key_grad, value_grad = attention_backward(
        queries, keys_bf, values_bf, attended, log_totals, attended_grad, segment_row
    )
    cosines, sines = rope_tables(length, head_width)
    projected_grad = jnp.stack(
        [
            rotate(query_grad, cosines, sines, -1.0),
            rotate(key_grad, cosines, sines, -1.0),
            value_grad,
        ],
        axis=1,
    )
    grad_bias = jnp.sum(projected_grad, axis=0)
    projected_cot = projected_grad.reshape(length, -1).astype(bf16)
    grad_qkv = jnp.dot(
        jnp.transpose(normed_one), projected_cot, preferred_element_type=f32
    ).reshape(qkv_full.shape)
    normed_one_part = jnp.dot(
        projected_cot, jnp.transpose(qkv_full.reshape(model_width, -1)), preferred_element_type=f32
    )
    normed_one_grad = lax.psum(normed_one_part.astype(jnp.bfloat16), "tensor").astype(jnp.float32)
    grad_gain_one, input_grad = norm_backward(normed_one_grad, input_f32, scale_one, gain_one)
    input_grad = input_grad + middle_grad
    own_grad = lax.dynamic_slice_in_dim(
        input_grad, lax.axis_index("tensor") * own_count, own_count, 0
    )
    all_shards = (
        lax.psum_scatter(grad_gain_one, "dp", scatter_dimension=0, tiled=True),
        lax.psum_scatter(grad_qkv, "dp", scatter_dimension=0, tiled=True),
        lax.psum_scatter(grad_bias, "dp", scatter_dimension=2, tiled=True),
        lax.psum_scatter(grad_out_weight, "dp", scatter_dimension=2, tiled=True),
        lax.psum_scatter(grad_gain_two, "dp", scatter_dimension=0, tiled=True),
        lax.psum_scatter(grad_shared_in, "dp", scatter_dimension=0, tiled=True),
        lax.psum_scatter(grad_shared_out, "dp", scatter_dimension=1, tiled=True),
        lax.psum_scatter(grad_gate, "dp", scatter_dimension=0, tiled=True),
    )
    attn_shards = all_shards[:4]
    ffn_shards = all_shards[4:]
    return (
        block_output,
        own_grad,
        attn_shards[0],
        attn_shards[1],
        attn_shards[2],
        attn_shards[3],
        ffn_shards[0],
        ffn_shards[1],
        ffn_shards[2],
        ffn_shards[3],
        expert_in_grad,
        expert_out_grad,
    )


def solution(mesh):
    placed = (
        P(("dp", "tensor"), None),
        P("dp"),
        P("dp", None, "tensor", None),
        P(None, "tensor", "dp"),
        P("tensor", None, "dp"),
        P("dp"),
        P("dp", None, "tensor"),
        P("tensor", "dp"),
        P("dp"),
        P("dp", None, None, "tensor"),
        P("dp", "tensor", None),
        P("dp", None),
        P("dp", None),
        P("dp", None),
        P(("dp", "tensor"), None),
    )
    returned = (
        P(("dp", "tensor"), None),
        P(("dp", "tensor"), None),
        P("dp"),
        P("dp", None, "tensor", None),
        P(None, "tensor", "dp"),
        P("tensor", None, "dp"),
        P("dp"),
        P("dp", None, "tensor"),
        P("tensor", "dp"),
        P("dp"),
        P("dp", None, None, "tensor"),
        P("dp", "tensor", None),
    )

    def step(*arrays):
        rows, width = arrays[0].shape
        fits = rows * width * arrays[0].dtype.itemsize <= gathered_limit
        plan = body if fits else body_by_slots
        return jax.shard_map(
            plan, mesh=mesh, in_specs=placed, out_specs=returned, check_vma=False
        )(*arrays)

    return step
```
